768 devices in a mesh: segment: 12 (over z), ctx: 16 (over x, y_hi, core), tp: 4 (over y_lo).
Axes of the slice: x: 4, y: 8 (y_hi: 2, y_lo: 4; y = y_hi * 4 + y_lo), z: 12, core: 2. Of those that a mesh axis runs over, the one named last changes fastest.
Arguments:
- hidden_in: bfloat16 [12, 2048, 4096], P('segment', 'ctx')
- norm_gain: bfloat16 [12, 4096], P('segment'), may hold values from 0.5 to 1.5
- query_weight: bfloat16 [12, 4096, 4096], P('segment', None, 'tp')
- keyval_weight: bfloat16 [12, 4096, 2048], P('segment', None, 'tp')
- output_weight: bfloat16 [12, 4096, 4096], P('segment', 'tp'), may hold values from -0.1875 to 0.1875
- windows: int32 [12], P('segment'), may hold values from 192 to 384, as said below
Outputs:
- handed: bfloat16 [12, 2048, 4096], P('segment', 'ctx', 'tp')
The draws below stay inside these ranges and needn't reach their ends.
Inputs may be any that keep to these rules, and one draw needn't show every extreme that they name: `windows`: one section's window is exactly 384 tokens.
All inputs are finite; a program needn't handle non-finite values.
Results may differ from the reference program's by a relative error of at most 0.006.
The reference program's roundings to bfloat16 on the way count: a program that leaves them out, or rounds other values in their place, can miss the bound.
Values may be sent and summed in bfloat16 or wider, within the bound.
A program may use at most 128 MiB of HBM per device.

```python
import math
import jax
import jax.numpy as jnp
from jax import lax

D = 4096
HD = 128
QHEADS = 32
KVHEADS = 8
TOKENS = 2048
WINMAX = 384
N_SEGMENT = 12


def feature_count():
    return min(64, D // 4)


def plant_scale():
    return math.sqrt(2000.0 / (0.9 * D * feature_count() * math.sqrt(HD)))


def draw_hidden_in(key, part):
    base_key, sink_key, strength_key, factor_key = jax.random.split(key, 4)
    shape = (N_SEGMENT, TOKENS, D)
    sinks = jax.random.uniform(sink_key, (N_SEGMENT, TOKENS, 1), jnp.float32) < 0.125
    base = jnp.clip(jax.random.normal(base_key, shape, jnp.float32), -6.0, 6.0)
    strength = jax.random.uniform(strength_key, (N_SEGMENT, TOKENS, 1), jnp.float32, 1.5, 3.0)
    factor = jax.random.uniform(factor_key, shape, jnp.float32, 0.8, 1.2)
    leading = (jnp.arange(D) < feature_count())[None, None, :]
    massive = strength * math.sqrt(D / feature_count()) * factor
    return jnp.where(sinks & leading, massive, base).astype(jnp.bfloat16)


def planted_weight(key, shape, chosen_columns):
    base_key, plant_key = jax.random.split(key)
    spread = D ** (-0.5)
    base = jnp.clip(jax.random.normal(base_key, shape, jnp.float32), -6.0, 6.0) * spread
    planted = plant_scale() * jax.random.uniform(plant_key, shape, jnp.float32, 0.8, 1.2)
    leading = (jnp.arange(D) < feature_count())[None, :, None]
    return jnp.where(leading & chosen_columns[None, None, :], planted, base).astype(jnp.bfloat16)


def draw_query_weight(key, part):
    column = jnp.arange(QHEADS * HD) % HD
    chosen = column % (HD // 2) >= HD // 2 - HD // 8
    return planted_weight(key, (N_SEGMENT, D, QHEADS * HD), chosen)


def draw_keyval_weight(key, part):
    column = jnp.arange(KVHEADS * 2 * HD) % (2 * HD)
    chosen = (column < HD) & (column % (HD // 2) >= HD // 2 - HD // 8)
    return planted_weight(key, (N_SEGMENT, D, KVHEADS * 2 * HD), chosen)


def draw_windows(key, part):
    first_key, second_key = jax.random.split(key)
    lengths = jax.random.randint(first_key, (N_SEGMENT,), WINMAX // 2, WINMAX + 1)
    chosen = jax.random.randint(second_key, (), 0, N_SEGMENT)
    return jnp.where(jnp.arange(N_SEGMENT) == chosen, WINMAX, lengths).astype(jnp.int32)


def steps_of(key, shape, cuts, smallest, top_value):
    loudness, own = 1.0, jax.random.fold_in(key, 6)
    for axis_at, blocks in cuts:
        heights = jnp.exp(jax.random.uniform(jax.random.fold_in(own, axis_at), (blocks,), jnp.float32, smallest / len(cuts), top_value / len(cuts)))
        loudness = loudness * jnp.repeat(heights, shape[axis_at] // blocks).reshape([-1 if axis == axis_at else 1 for axis in range(len(shape))])
    return loudness


def noise(own_key, dims, deviation, bound, cuts=(), kind=jnp.bfloat16):
    values = jax.random.normal(own_key, dims, jnp.float32) * deviation
    if len(cuts) > 0:
        values = steps_of(own_key, dims, cuts, -0.22, 0.18) * values
    return jnp.clip(values, min=-bound, max=bound).astype(kind)


def setup_inputs(seed: int = 0) -> dict:
    seeds = jax.random.split(jax.random.key(seed), 7)
    hidden_in = draw_hidden_in(jax.random.fold_in(seeds[6], 71), 0)
    norm_gain = jnp.clip(1.0 + 0.1 * jax.random.normal(seeds[1], (N_SEGMENT, D), jnp.float32), 0.5, 1.5).astype(jnp.bfloat16)
    query_weight = draw_query_weight(jax.random.fold_in(seeds[6], 71), 0)
    keyval_weight = draw_keyval_weight(jax.random.fold_in(seeds[6], 71), 0)
    output_weight = noise(seeds[4], (N_SEGMENT, QHEADS * HD, D), (QHEADS * HD // 4) ** -0.5, 0.1875, ((0, 12), (1, 4)))
    windows = draw_windows(jax.random.fold_in(seeds[6], 71), 0)
    return {"hidden_in": hidden_in, "norm_gain": norm_gain, "query_weight": query_weight, "keyval_weight": keyval_weight, "output_weight": output_weight, "windows": windows}


NORM_EPS = 1e-05

def rotate(vector, positions):
    half_dim = vector.shape[-1] // 2
    inverse = 10000.0 ** (-jnp.arange(half_dim, dtype=jnp.float32) / half_dim)
    angles = positions.astype(jnp.float32)[:, None, None] * inverse[None, None, :]
    cosine = jnp.cos(angles)
    sine = jnp.sin(angles)
    first_half = vector[..., :half_dim]
    second_half = vector[..., half_dim:]
    return jnp.concatenate([first_half * cosine - second_half * sine, second_half * cosine + first_half * sine], axis=-1)

def attend(queries, keys, values, query_pos, key_pos, width):
    scores = jnp.einsum('qgd,kd->gqk', queries.astype(jnp.float32), keys.astype(jnp.float32)) * HD ** (-0.5)
    distance = query_pos[:, None] - key_pos[None, :]
    inside = ((distance >= 0) & (distance < width) & (key_pos[None, :] >= 0))[None]
    scores = jnp.where(inside, scores, jnp.float32(-1e+30))
    highest = lax.optimization_barrier(jnp.max(scores, axis=2, keepdims=True))
    expo = jnp.where(inside, jnp.exp(scores - highest), jnp.float32(0.0))
    probs = (expo / lax.optimization_barrier(jnp.sum(expo, axis=2, keepdims=True))).astype(jnp.bfloat16)
    return jnp.einsum('gqk,kd->qgd', probs.astype(jnp.float32), values.astype(jnp.float32)).astype(jnp.bfloat16)

def normalize(token_rows, gain_row):
    wide_rows = token_rows.astype(jnp.float32)
    mean_square = lax.optimization_barrier(jnp.mean(wide_rows * wide_rows, axis=1, keepdims=True))
    return (wide_rows * lax.rsqrt(mean_square + NORM_EPS) * gain_row.astype(jnp.float32)[None, :]).astype(jnp.bfloat16)

def reference(hidden_in, norm_gain, query_weight, keyval_weight, output_weight, windows):
    positions = jnp.arange(TOKENS, dtype=jnp.int32)
    group = QHEADS // KVHEADS
    blocks = []
    for section in range(N_SEGMENT):
        normed = normalize(hidden_in[section], norm_gain[section])
        key_value = jnp.dot(normed, keyval_weight[section], preferred_element_type=jnp.float32).reshape(TOKENS, KVHEADS, 2, HD)
        keys = rotate(key_value[:, :, 0], positions).astype(jnp.bfloat16)
        values = key_value[:, :, 1].astype(jnp.bfloat16)
        queries = jnp.dot(normed, query_weight[section], preferred_element_type=jnp.float32).reshape(TOKENS, QHEADS, HD)
        queries = rotate(queries, positions).astype(jnp.bfloat16)
        outs_list = []
        for kv_index in range(KVHEADS):
            outs_list.append(attend(queries[:, kv_index * group:(kv_index + 1) * group], keys[:, kv_index], values[:, kv_index], positions, positions, windows[section]))
        attn = jnp.concatenate(outs_list, axis=1).reshape(TOKENS, QHEADS * HD)
        blocks.append(jnp.dot(attn, output_weight[section], preferred_element_type=jnp.float32).astype(jnp.bfloat16))
    stacked = jnp.stack(blocks)
    return jnp.roll(stacked, 1, axis=0)
```

```python
import functools

import jax
import jax.numpy as jnp
from jax import lax
from jax.experimental import pallas as pl
from jax.experimental.pallas import tpu as pltpu
from jax.sharding import PartitionSpec as P

HD = 128
NORM_EPS = 1e-05
MESH = pl.DeviceIdType.MESH
LOG2E = 1.4426950408889634


def block_kernel(
    n_seg,
    n_ctx,
    n_tp,
    win_ref,
    gain_ref,
    inv_ref,
    hid_hbm,
    wkv_hbm,
    wq_hbm,
    wo_hbm,
    out_hbm,
    hid,
    wkv,
    wq,
    wo,
    normed,
    kv,
    query,
    attn,
    part,
    landed,
    final,
    load_sem,
    kv_send,
    kv_recv,
    rs_send,
    rs_recv,
    z_send,
    z_recv,
):
    seg = lax.axis_index("segment")
    ctx = lax.axis_index("ctx")
    tp = lax.axis_index("tp")
    rows, width = hid.shape
    heads = query.shape[0]
    groups = kv.shape[2] // (2 * HD)
    per_group = heads // groups
    cols = part.shape[2]

    loads = [
        pltpu.make_async_copy(hid_hbm.at[0], hid, load_sem.at[0]),
        pltpu.make_async_copy(wkv_hbm.at[0], wkv, load_sem.at[1]),
        pltpu.make_async_copy(wq_hbm.at[0], wq, load_sem.at[2]),
        pltpu.make_async_copy(wo_hbm.at[0], wo, load_sem.at[3]),
    ]
    for load in loads:
        load.start()

    def at_ctx(steps):
        return {"ctx": lax.rem(ctx + steps + n_ctx, n_ctx)}

    core = lax.rem(ctx, 2)
    partner = {"ctx": ctx + 1 - 2 * core}

    barrier = pltpu.get_barrier_semaphore()
    peers = [partner]
    peers += [at_ctx(steps) for steps in (2, -2, 3, -3)]
    peers += [{"tp": lax.rem(tp + step, n_tp)} for step in range(1, n_tp)]
    peers += [
        {"segment": lax.rem(seg + 1, n_seg)},
        {"segment": lax.rem(seg + n_seg - 1, n_seg)},
    ]
    for peer in peers:
        pl.semaphore_signal(barrier, inc=1, device_id=peer, device_id_type=MESH)

    row_at = lax.broadcasted_iota(jnp.int32, (rows, HD), 0)
    lane_at = lax.broadcasted_iota(jnp.int32, (rows, HD), 1)
    angles = (ctx * rows + row_at).astype(jnp.float32) * inv_ref[...]
    cosine = jnp.cos(angles)
    sine = jnp.where(lane_at < HD // 2, -jnp.sin(angles), jnp.sin(angles))

    def rope(vector):
        return vector * cosine + pltpu.roll(vector, HD // 2, 1) * sine

    loads[0].wait()
    gain = gain_ref[...].astype(jnp.float32)
    for first in range(0, rows, 16):
        wide = hid[first : first + 16, :].astype(jnp.float32)
        scale = lax.rsqrt(jnp.sum(wide * wide, axis=1, keepdims=True) * (1.0 / width) + NORM_EPS)
        normed[first : first + 16, :] = (wide * scale * gain).astype(jnp.bfloat16)

    loads[1].wait()
    for group in range(groups):
        low = group * 2 * HD
        both = jnp.dot(
            normed[...], wkv[:, low : low + 2 * HD], preferred_element_type=jnp.float32
        )
        kv[0, :, low : low + HD] = rope(both[:, :HD]).astype(jnp.bfloat16)
        kv[0, :, low + HD : low + 2 * HD] = both[:, HD:].astype(jnp.bfloat16)

    pl.semaphore_wait(barrier, len(peers))

    def send_kv(source, slot, target, sem):
        return pltpu.make_async_remote_copy(
            src_ref=kv.at[source],
            dst_ref=kv.at[slot],
            send_sem=kv_send.at[sem],
            recv_sem=kv_recv.at[slot],
            device_id=target,
            device_id_type=MESH,
        )

    across = send_kv(0, 2, at_ctx(2), 0)
    across.start()

    @pl.when(core == 0)
    def _():
        send_kv(0, 1, partner, 1).start()

    @pl.when(core == 1)
    def _():
        send_kv(0, 3, at_ctx(3), 1).start()

    loads[2].wait()

    for pair in range(heads // 2):
        both = jnp.dot(
            normed[...],
            wq[:, pair * 2 * HD : (pair + 1) * 2 * HD],
            preferred_element_type=jnp.float32,
        )
        query[2 * pair] = rope(both[:, :HD]).astype(jnp.bfloat16)
        query[2 * pair + 1] = rope(both[:, HD:]).astype(jnp.bfloat16)

    across.wait_recv()

    @pl.when(core == 0)
    def _():
        send_kv(2, 3, partner, 2).start()

    @pl.when(core == 1)
    def _():
        send_kv(2, 1, partner, 2).start()

    send_kv(0, 1, partner, 1).wait_recv()
    send_kv(0, 3, partner, 2).wait_recv()

    window = win_ref[0]
    biases = []
    for slot in range(4):
        distance = row_at - lane_at + slot * rows
        inside = (distance >= 0) & (distance < window) & (ctx >= slot)
        biases.append(jnp.where(inside, jnp.float32(0.0), jnp.float32(-1e30)))

    for head in range(heads):
        low = (head // per_group) * 2 * HD
        scores = []
        for slot in range(4):
            scores.append(
                lax.dot_general(
                    query[head],
                    kv[slot, :, low : low + HD],
                    (((1,), (1,)), ((), ())),
                    preferred_element_type=jnp.float32,
                )
                + biases[slot]
            )
        highest = jnp.max(
            jnp.maximum(
                jnp.maximum(scores[0], scores[1]), jnp.maximum(scores[2], scores[3])
            ),
            axis=1,
            keepdims=True,
        )
        expo = [jnp.exp2((score - highest) * (HD**-0.5 * LOG2E)) for score in scores]
        total = jnp.sum((expo[0] + expo[1]) + (expo[2] + expo[3]), axis=1, keepdims=True)
        inverse = 1.0 / total
        mixed = None
        for slot in range(4):
            term = jnp.dot(
                (expo[slot] * inverse).astype(jnp.bfloat16),
                kv[slot, :, low + HD : low + 2 * HD],
                preferred_element_type=jnp.float32,
            )
            mixed = term if mixed is None else mixed + term
        attn[:, head * HD : (head + 1) * HD] = mixed.astype(jnp.bfloat16)

    loads[3].wait()

    def share(target):
        low = pl.multiple_of(target * cols, cols)
        return jnp.dot(
            attn[...], wo[:, pl.ds(low, cols)], preferred_element_type=jnp.float32
        )

    sends = []
    for step in range(1, n_tp):
        target = lax.rem(tp + step, n_tp)
        part[step - 1] = share(target).astype(jnp.bfloat16)
        send = pltpu.make_async_remote_copy(
            src_ref=part.at[step - 1],
            dst_ref=landed.at[step - 1],
            send_sem=rs_send.at[step - 1],
            recv_sem=rs_recv.at[step - 1],
            device_id={"tp": target},
            device_id_type=MESH,
        )
        send.start()
        sends.append(send)
    own = share(tp)
    for send in sends:
        send.wait_recv()
    for step in range(n_tp - 1):
        own = own + landed[step].astype(jnp.float32)
    final[...] = own.astype(jnp.bfloat16)
    hand = pltpu.make_async_remote_copy(
        src_ref=final,
        dst_ref=out_hbm.at[0],
        send_sem=z_send,
        recv_sem=z_recv,
        device_id={"segment": lax.rem(seg + 1, n_seg)},
        device_id_type=MESH,
    )
    hand.start()
    across.wait_send()
    send_kv(0, 1, partner, 1).wait_send()
    send_kv(2, 1, partner, 2).wait_send()
    for send in sends:
        send.wait_send()
    hand.wait()


def solution(mesh):
    n_seg, n_ctx, n_tp = mesh.shape["segment"], mesh.shape["ctx"], mesh.shape["tp"]

    def body(hidden_in, norm_gain, query_weight, keyval_weight, output_weight, windows):
        rows, width = hidden_in.shape[1:]
        heads = query_weight.shape[2] // HD
        cols = output_weight.shape[2] // n_tp
        half = HD // 2
        inverse = 10000.0 ** (-jnp.arange(half, dtype=jnp.float32) / half)
        inverse = jnp.concatenate([inverse, inverse])[None, :]
        bf16 = jnp.bfloat16
        vmem = pl.BlockSpec(memory_space=pltpu.VMEM)
        hbm = pl.BlockSpec(memory_space=pl.ANY)
        return pl.pallas_call(
            functools.partial(block_kernel, n_seg, n_ctx, n_tp),
            out_shape=jax.ShapeDtypeStruct((1, rows, cols), bf16),
            in_specs=[pl.BlockSpec(memory_space=pltpu.SMEM), vmem, vmem, hbm, hbm, hbm, hbm],
            out_specs=hbm,
            scratch_shapes=[
                pltpu.VMEM((rows, width), bf16),
                pltpu.VMEM(keyval_weight.shape[1:], bf16),
                pltpu.VMEM(query_weight.shape[1:], bf16),
                pltpu.VMEM(output_weight.shape[1:], bf16),
                pltpu.VMEM((rows, width), bf16),
                pltpu.VMEM((4, rows, keyval_weight.shape[2]), bf16),
                pltpu.VMEM((heads, rows, HD), bf16),
                pltpu.VMEM((rows, heads * HD), bf16),
                pltpu.VMEM((n_tp - 1, rows, cols), bf16),
                pltpu.VMEM((n_tp - 1, rows, cols), bf16),
                pltpu.VMEM((rows, cols), bf16),
                pltpu.SemaphoreType.DMA((4,)),
                pltpu.SemaphoreType.DMA((3,)),
                pltpu.SemaphoreType.DMA((4,)),
                pltpu.SemaphoreType.DMA((n_tp - 1,)),
                pltpu.SemaphoreType.DMA((n_tp - 1,)),
                pltpu.SemaphoreType.DMA,
                pltpu.SemaphoreType.DMA,
            ],
            compiler_params=pltpu.CompilerParams(
                collective_id=0, has_side_effects=True, vmem_limit_bytes=56 * 1024 * 1024
            ),
        )(
            windows,
            norm_gain,
            inverse,
            hidden_in,
            keyval_weight,
            query_weight,
            output_weight,
        )

    in_specs = (
        P("segment", "ctx", None),
        P("segment", None),
        P("segment", None, "tp"),
        P("segment", None, "tp"),
        P("segment", "tp", None),
        P("segment"),
    )
    out_specs = P("segment", "ctx", "tp")
    return jax.shard_map(body, mesh=mesh, in_specs=in_specs, out_specs=out_specs, check_vma=False)
```

```python
import functools

import jax
import jax.numpy as jnp
import numpy as np
from jax import lax
from jax.experimental import pallas as pl
from jax.experimental.pallas import tpu as pltpu
from jax.sharding import PartitionSpec as P

HD = 128
PIECE = 32
NORM_EPS = 1e-05
MESH = pl.DeviceIdType.MESH
LOG2E = 1.4426950408889634


def block_kernel(
    n_seg,
    n_ctx,
    n_tp,
    piece,
    win_ref,
    gain_ref,
    inv_ref,
    hid_hbm,
    wkv_hbm,
    wq_hbm,
    wo_hbm,
    out_hbm,
    hid,
    wkv,
    wq,
    wo,
    normed,
    kv,
    query,
    attn,
    bias,
    own,
    part,
    from_outer,
    from_inner,
    final,
    load_sem,
    kv_send,
    kv_recv,
    rs_send,
    outer_recv,
    inner_recv,
    z_send,
    z_recv,
):
    seg = lax.axis_index("segment")
    ctx = lax.axis_index("ctx")
    tp = lax.axis_index("tp")
    rows, width = hid.shape
    heads = query.shape[0]
    groups = kv.shape[1]
    per_group = heads // groups
    cols = part.shape[2]

    loads = [
        pltpu.make_async_copy(hid_hbm.at[0], hid, load_sem.at[0]),
        pltpu.make_async_copy(wkv_hbm.at[0], wkv, load_sem.at[1]),
        pltpu.make_async_copy(wq_hbm.at[0], wq, load_sem.at[2]),
        pltpu.make_async_copy(wo_hbm.at[0], wo, load_sem.at[3]),
    ]
    loads[0].start()
    loads[1].start()

    def at_ctx(steps):
        return {"ctx": lax.rem(ctx + steps + n_ctx, n_ctx)}

    core = lax.rem(ctx, 2)
    partner = {"ctx": ctx + 1 - 2 * core}
    half = tp // 2
    inward = {"tp": tp + 1 - 2 * half}
    at_end = lax.rem(tp, 3) == 0

    barrier = pltpu.get_barrier_semaphore()
    peers = [partner]
    peers += [at_ctx(steps) for steps in (2, -2, 3, -3)]
    peers += [{"tp": lax.rem(tp + step, n_tp)} for step in range(1, n_tp)]
    peers += [
        {"segment": lax.rem(seg + 1, n_seg)},
        {"segment": lax.rem(seg + n_seg - 1, n_seg)},
    ]
    for peer in peers:
        pl.semaphore_signal(barrier, inc=1, device_id=peer, device_id_type=MESH)

    row_at = lax.broadcasted_iota(jnp.int32, (rows, HD), 0)
    lane_at = lax.broadcasted_iota(jnp.int32, (rows, HD), 1)
    angles = (ctx * rows + row_at).astype(jnp.float32) * inv_ref[...]
    cosine = jnp.cos(angles)
    sine = jnp.sin(angles)
    sine = jnp.where(lane_at < HD // 2, -sine, sine)

    def rope(vector):
        return vector * cosine + pltpu.roll(vector, HD // 2, 1) * sine

    loads[0].wait()
    loads[2].start()
    loads[3].start()
    gain = gain_ref[...].astype(jnp.float32)
    for first in range(0, rows, 16):
        wide = hid[first : first + 16, :].astype(jnp.float32)
        scale = lax.rsqrt(jnp.sum(wide * wide, axis=1, keepdims=True) * (1.0 / width) + NORM_EPS)
        normed[first : first + 16, :] = (wide * scale * gain).astype(jnp.bfloat16)

    def send_kv(source, slot, group, target, sem):
        return pltpu.make_async_remote_copy(
            src_ref=kv.at[source, group],
            dst_ref=kv.at[slot, group],
            send_sem=kv_send.at[sem, group],
            recv_sem=kv_recv.at[slot, group],
            device_id=target,
            device_id_type=MESH,
        )

    loads[1].wait()
    for group in range(groups):
        low = group * 2 * HD
        both = jnp.dot(
            normed[...], wkv[:, low : low + 2 * HD], preferred_element_type=jnp.float32
        )
        kv[0, group, :, :HD] = rope(both[:, :HD]).astype(jnp.bfloat16)
        kv[0, group, :, HD:] = both[:, HD:].astype(jnp.bfloat16)
        if group == 0:
            pl.semaphore_wait(barrier, len(peers))
        send_kv(0, 2, group, at_ctx(2), 0).start()

        @pl.when(core == 0)
        def _():
            send_kv(0, 1, group, partner, 1).start()

        @pl.when(core == 1)
        def _():
            send_kv(0, 3, group, at_ctx(3), 1).start()

    loads[2].wait()

    for pair in range(heads // 2):
        both = jnp.dot(
            normed[...],
            wq[:, pair * 2 * HD : (pair + 1) * 2 * HD],
            preferred_element_type=jnp.float32,
        )
        query[2 * pair] = rope(both[:, :HD]).astype(jnp.bfloat16)
        query[2 * pair + 1] = rope(both[:, HD:]).astype(jnp.bfloat16)

    window = win_ref[0]
    for slot in range(4):
        distance = row_at - lane_at + slot * rows
        inside = (distance >= 0) & (distance < window) & (ctx >= slot)
        bias[slot] = jnp.where(inside, jnp.float32(0.0), jnp.float32(-1e30))

    for group in range(groups):
        send_kv(0, 2, group, partner, 0).wait_recv()

        @pl.when(core == 0)
        def _():
            send_kv(2, 3, group, partner, 2).start()

        @pl.when(core == 1)
        def _():
            send_kv(2, 1, group, partner, 2).start()

    for group in range(groups):
        send_kv(0, 1, group, partner, 1).wait_recv()
        send_kv(0, 3, group, partner, 2).wait_recv()
        for head in range(group * per_group, (group + 1) * per_group):
            scores = []
            for slot in range(4):
                scores.append(
                    lax.dot_general(
                        query[head],
                        kv[slot, group, :, :HD],
                        (((1,), (1,)), ((), ())),
                        preferred_element_type=jnp.float32,
                    )
                    + bias[slot]
                )
            highest = jnp.max(
                jnp.maximum(
                    jnp.maximum(scores[0], scores[1]), jnp.maximum(scores[2], scores[3])
                ),
                axis=1,
                keepdims=True,
            )
            expo = [jnp.exp2((score - highest) * (HD**-0.5 * LOG2E)) for score in scores]
            total = jnp.sum((expo[0] + expo[1]) + (expo[2] + expo[3]), axis=1, keepdims=True)
            inverse = 1.0 / total
            mixed = None
            for slot in range(4):
                term = jnp.dot(
                    (expo[slot] * inverse).astype(jnp.bfloat16),
                    kv[slot, group, :, HD:],
                    preferred_element_type=jnp.float32,
                )
                mixed = term if mixed is None else mixed + term
            attn[:, head * HD : (head + 1) * HD] = mixed.astype(jnp.bfloat16)

    loads[3].wait()

    def send_part(index, at, place, sem, target):
        band = pl.ds(at * piece, piece)
        return pltpu.make_async_remote_copy(
            src_ref=part.at[index, band],
            dst_ref=place.at[band],
            send_sem=rs_send.at[index, at],
            recv_sem=sem.at[at],
            device_id=target,
            device_id_type=MESH,
        )

    def to_inner(index, at):
        return send_part(index, at, from_outer.at[index], outer_recv.at[index], inward)

    def over_middle(index, at):
        return send_part(index, at, from_inner.at[index], inner_recv.at[index], inward)

    def to_end(at):
        outward = {"tp": tp - 1 + 2 * half}
        return send_part(2, at, from_inner.at[0], inner_recv.at[0], outward)

    def hand(at):
        band = pl.ds(at * piece, piece)
        return pltpu.make_async_remote_copy(
            src_ref=final.at[band],
            dst_ref=out_hbm.at[0, band],
            send_sem=z_send.at[at],
            recv_sem=z_recv.at[at],
            device_id={"segment": lax.rem(seg + 1, n_seg)},
            device_id_type=MESH,
        )

    f32 = jnp.float32
    bands = rows // piece
    for step in range(4):
        mirrored = 3 - step
        low = pl.multiple_of((mirrored + half * (3 - 2 * mirrored)) * cols, cols)
        share = jnp.dot(attn[...], wo[:, pl.ds(low, cols)], preferred_element_type=f32)
        own[step] = share
        if step < 3:

            @pl.when(at_end)
            def _():
                part[step] = share.astype(jnp.bfloat16)
                for at in range(bands):
                    to_inner(step, at).start()

    def finish(at, terms):
        band = slice(at * piece, (at + 1) * piece)
        total = terms[0][band]
        for term in terms[1:]:
            total = total + term[band].astype(f32)
        final[band] = total.astype(jnp.bfloat16)
        hand(at).start()

    def add_on(index, at, mine, landed):
        band = slice(at * piece, (at + 1) * piece)
        part[index, band] = (mine[band] + landed[band].astype(f32)).astype(jnp.bfloat16)

    @pl.when(at_end)
    def _():
        for at in range(bands):
            to_end(at).wait_recv()
            finish(at, [own.at[3], from_inner.at[0]])
        for step in range(3):
            for at in range(bands):
                to_inner(step, at).wait_send()

    @pl.when(jnp.logical_not(at_end))
    def _():
        for at in range(bands):
            to_inner(0, at).wait_recv()
            add_on(0, at, own.at[0], from_outer.at[0])
            over_middle(0, at).start()
        for at in range(bands):
            to_inner(1, at).wait_recv()
            add_on(1, at, own.at[1], from_outer.at[1])
            over_middle(1, at).start()
            over_middle(0, at).wait_recv()
            add_on(2, at, own.at[3], from_inner.at[0])
            to_end(at).start()
        for at in range(bands):
            to_inner(2, at).wait_recv()
            over_middle(1, at).wait_recv()
            finish(at, [own.at[2], from_outer.at[2], from_inner.at[1]])
        for at in range(bands):
            over_middle(0, at).wait_send()
            over_middle(1, at).wait_send()
            to_end(at).wait_send()

    for group in range(groups):
        send_kv(0, 2, group, partner, 0).wait_send()
        send_kv(0, 1, group, partner, 1).wait_send()
        send_kv(2, 1, group, partner, 2).wait_send()
    for at in range(bands):
        hand(at).wait()


def solution(mesh):
    n_seg, n_ctx, n_tp = mesh.shape["segment"], mesh.shape["ctx"], mesh.shape["tp"]

    def body(hidden_in, norm_gain, query_weight, keyval_weight, output_weight, windows):
        rows, width = hidden_in.shape[1:]
        heads = query_weight.shape[2] // HD
        cols = output_weight.shape[2] // n_tp
        groups = keyval_weight.shape[2] // (2 * HD)
        bands = rows // PIECE
        half = HD // 2
        inverse = 10000.0 ** (-np.arange(half) / half)
        inverse = jnp.asarray(np.tile(inverse, 2)[None, :], dtype=jnp.float32)
        bf16 = jnp.bfloat16
        vmem = pl.BlockSpec(memory_space=pltpu.VMEM)
        hbm = pl.BlockSpec(memory_space=pl.ANY)
        return pl.pallas_call(
            functools.partial(block_kernel, n_seg, n_ctx, n_tp, PIECE),
            out_shape=jax.ShapeDtypeStruct((1, rows, cols), bf16),
            in_specs=[pl.BlockSpec(memory_space=pltpu.SMEM), vmem, vmem, hbm, hbm, hbm, hbm],
            out_specs=hbm,
            scratch_shapes=[
                pltpu.VMEM((rows, width), bf16),
                pltpu.VMEM(keyval_weight.shape[1:], bf16),
                pltpu.VMEM(query_weight.shape[1:], bf16),
                pltpu.VMEM(output_weight.shape[1:], bf16),
                pltpu.VMEM((rows, width), bf16),
                pltpu.VMEM((4, groups, rows, 2 * HD), bf16),
                pltpu.VMEM((heads, rows, HD), bf16),
                pltpu.VMEM((rows, heads * HD), bf16),
                pltpu.VMEM((4, rows, HD), jnp.float32),
                pltpu.VMEM((4, rows, cols), jnp.float32),
                pltpu.VMEM((3, rows, cols), bf16),
                pltpu.VMEM((3, rows, cols), bf16),
                pltpu.VMEM((2, rows, cols), bf16),
                pltpu.VMEM((rows, cols), bf16),
                pltpu.SemaphoreType.DMA((4,)),
                pltpu.SemaphoreType.DMA((3, groups)),
                pltpu.SemaphoreType.DMA((4, groups)),
                pltpu.SemaphoreType.DMA((3, bands)),
                pltpu.SemaphoreType.DMA((3, bands)),
                pltpu.SemaphoreType.DMA((2, bands)),
                pltpu.SemaphoreType.DMA((bands,)),
                pltpu.SemaphoreType.DMA((bands,)),
            ],
            compiler_params=pltpu.CompilerParams(
                collective_id=0, has_side_effects=True, vmem_limit_bytes=56 * 1024 * 1024
            ),
        )(
            windows,
            norm_gain,
            inverse,
            hidden_in,
            keyval_weight,
            query_weight,
            output_weight,
        )

    in_specs = (
        P("segment", "ctx", None),
        P("segment", None),
        P("segment", None, "tp"),
        P("segment", None, "tp"),
        P("segment", "tp", None),
        P("segment"),
    )
    out_specs = P("segment", "ctx", "tp")
    return jax.shard_map(body, mesh=mesh, in_specs=in_specs, out_specs=out_specs, check_vma=False)
```

```python
import functools

import jax
import jax.numpy as jnp
import numpy as np
from jax import lax
from jax.experimental import pallas as pl
from jax.experimental.pallas import tpu as pltpu
from jax.sharding import PartitionSpec as P

HD = 128
PIECE = 16
DEPTHS = 4
NORM_EPS = 1e-05
MESH = pl.DeviceIdType.MESH
LOG2E = 1.4426950408889634


def block_kernel(
    n_seg,
    n_ctx,
    n_tp,
    piece,
    win_ref,
    gain_hbm,
    inv_hbm,
    hid_hbm,
    wkv_hbm,
    wq_hbm,
    wo_hbm,
    out_ref,
    gain_row,
    inv_row,
    hid,
    wkv,
    wq,
    wo,
    normed,
    kv,
    query,
    attn,
    bias,
    own,
    part,
    from_outer,
    from_inner,
    final,
    load_sem,
    kv_send,
    kv_recv,
    rs_send,
    outer_recv,
    inner_recv,
    z_send,
    z_recv,
):
    seg = lax.axis_index("segment")
    ctx = lax.axis_index("ctx")
    tp = lax.axis_index("tp")
    rows, width = hid.shape
    heads = query.shape[0]
    groups = kv.shape[1]
    per_group = heads // groups
    cols = part.shape[2]

    depth = width // DEPTHS
    small = [
        pltpu.make_async_copy(inv_hbm, inv_row, load_sem.at[0]),
        pltpu.make_async_copy(gain_hbm, gain_row, load_sem.at[1]),
    ]
    load_hid = pltpu.make_async_copy(hid_hbm.at[0], hid, load_sem.at[2])
    load_wq = pltpu.make_async_copy(wq_hbm.at[0], wq, load_sem.at[3])
    load_wo = pltpu.make_async_copy(wo_hbm.at[0], wo, load_sem.at[4])
    load_wkv = []
    for at in range(DEPTHS):
        band = pl.ds(at * depth, depth)
        load_wkv.append(
            pltpu.make_async_copy(wkv_hbm.at[0, band], wkv.at[band], load_sem.at[5 + at])
        )
    for load in small + [load_hid] + load_wkv:
        load.start()

    def at_ctx(steps):
        return {"ctx": lax.rem(ctx + steps + n_ctx, n_ctx)}

    core = lax.rem(ctx, 2)
    partner = {"ctx": ctx + 1 - 2 * core}
    half = tp // 2
    inward = {"tp": tp + 1 - 2 * half}
    at_end = lax.rem(tp, 3) == 0

    barrier = pltpu.get_barrier_semaphore()
    peers = [partner]
    peers += [at_ctx(steps) for steps in (2, -2, 3, -3)]
    peers += [{"tp": lax.rem(tp + step, n_tp)} for step in range(1, n_tp)]
    peers += [
        {"segment": lax.rem(seg + 1, n_seg)},
        {"segment": lax.rem(seg + n_seg - 1, n_seg)},
    ]
    for peer in peers:
        pl.semaphore_signal(barrier, inc=1, device_id=peer, device_id_type=MESH)

    small[0].wait()
    row_at = lax.broadcasted_iota(jnp.int32, (rows, HD), 0)
    lane_at = lax.broadcasted_iota(jnp.int32, (rows, HD), 1)
    angles = (ctx * rows + row_at).astype(jnp.float32) * inv_row[...]
    cosine = jnp.cos(angles)
    sine = jnp.sin(angles)
    sine = jnp.where(lane_at < HD // 2, -sine, sine)

    def rope(vector):
        return vector * cosine + pltpu.roll(vector, HD // 2, 1) * sine

    small[1].wait()
    load_hid.wait()
    gain = gain_row[...].astype(jnp.float32)
    for first in range(0, rows, 16):
        wide = hid[first : first + 16, :].astype(jnp.float32)
        scale = lax.rsqrt(jnp.sum(wide * wide, axis=1, keepdims=True) * (1.0 / width) + NORM_EPS)
        normed[first : first + 16, :] = (wide * scale * gain).astype(jnp.bfloat16)

    def send_kv(source, slot, group, target, sem):
        return pltpu.make_async_remote_copy(
            src_ref=kv.at[source, group],
            dst_ref=kv.at[slot, group],
            send_sem=kv_send.at[sem, group],
            recv_sem=kv_recv.at[slot, group],
            device_id=target,
            device_id_type=MESH,
        )

    both = None
    for at in range(DEPTHS):
        band = slice(at * depth, (at + 1) * depth)
        load_wkv[at].wait()
        term = jnp.dot(normed[:, band], wkv[band, :], preferred_element_type=jnp.float32)
        both = term if both is None else both + term
    for group in range(groups):
        low = group * 2 * HD
        kv[0, group, :, :HD] = rope(both[:, low : low + HD]).astype(jnp.bfloat16)
        kv[0, group, :, HD:] = both[:, low + HD : low + 2 * HD].astype(jnp.bfloat16)
    pl.semaphore_wait(barrier, len(peers))
    for group in range(groups):
        send_kv(0, 2, group, at_ctx(2), 0).start()

        @pl.when(core == 0)
        def _():
            send_kv(0, 1, group, partner, 1).start()

        @pl.when(core == 1)
        def _():
            send_kv(0, 3, group, at_ctx(3), 1).start()

    load_wq.start()
    load_wo.start()
    load_wq.wait()

    for pair in range(heads // 2):
        both = jnp.dot(
            normed[...],
            wq[:, pair * 2 * HD : (pair + 1) * 2 * HD],
            preferred_element_type=jnp.float32,
        )
        query[2 * pair] = rope(both[:, :HD]).astype(jnp.bfloat16)
        query[2 * pair + 1] = rope(both[:, HD:]).astype(jnp.bfloat16)

    window = win_ref[0]
    for slot in range(4):
        distance = row_at - lane_at + slot * rows
        inside = (distance >= 0) & (distance < window) & (ctx >= slot)
        bias[slot] = jnp.where(inside, jnp.float32(0.0), jnp.float32(-1e30))

    for group in range(groups):
        send_kv(0, 2, group, partner, 0).wait_recv()

        @pl.when(core == 0)
        def _():
            send_kv(2, 3, group, partner, 2).start()

        @pl.when(core == 1)
        def _():
            send_kv(2, 1, group, partner, 2).start()

    for group in range(groups):
        send_kv(0, 1, group, partner, 1).wait_recv()
        send_kv(0, 3, group, partner, 2).wait_recv()
        for head in range(group * per_group, (group + 1) * per_group):
            scores = []
            for slot in range(4):
                scores.append(
                    lax.dot_general(
                        query[head],
                        kv[slot, group, :, :HD],
                        (((1,), (1,)), ((), ())),
                        preferred_element_type=jnp.float32,
                    )
                    + bias[slot]
                )
            highest = jnp.max(
                jnp.maximum(
                    jnp.maximum(scores[0], scores[1]), jnp.maximum(scores[2], scores[3])
                ),
                axis=1,
                keepdims=True,
            )
            expo = [jnp.exp2((score - highest) * (HD**-0.5 * LOG2E)) for score in scores]
            total = jnp.sum((expo[0] + expo[1]) + (expo[2] + expo[3]), axis=1, keepdims=True)
            inverse = 1.0 / total
            mixed = None
            for slot in range(4):
                term = jnp.dot(
                    (expo[slot] * inverse).astype(jnp.bfloat16),
                    kv[slot, group, :, HD:],
                    preferred_element_type=jnp.float32,
                )
                mixed = term if mixed is None else mixed + term
            attn[:, head * HD : (head + 1) * HD] = mixed.astype(jnp.bfloat16)

    load_wo.wait()

    def send_part(index, at, place, sem, target):
        band = pl.ds(at * piece, piece)
        return pltpu.make_async_remote_copy(
            src_ref=part.at[index, band],
            dst_ref=place.at[band],
            send_sem=rs_send.at[index, at],
            recv_sem=sem.at[at],
            device_id=target,
            device_id_type=MESH,
        )

    def to_inner(index, at):
        return send_part(index, at, from_outer.at[index], outer_recv.at[index], inward)

    def over_middle(index, at):
        return send_part(index, at, from_inner.at[index], inner_recv.at[index], inward)

    def to_end(at):
        outward = {"tp": tp - 1 + 2 * half}
        return send_part(2, at, from_inner.at[0], inner_recv.at[0], outward)

    def hand(at):
        band = pl.ds(at * piece, piece)
        return pltpu.make_async_remote_copy(
            src_ref=final.at[band],
            dst_ref=out_ref.at[0, band],
            send_sem=z_send.at[at],
            recv_sem=z_recv.at[at],
            device_id={"segment": lax.rem(seg + 1, n_seg)},
            device_id_type=MESH,
        )

    f32 = jnp.float32
    bands = rows // piece
    for step in range(4):
        mirrored = 3 - step
        low = pl.multiple_of((mirrored + half * (3 - 2 * mirrored)) * cols, cols)
        share = jnp.dot(attn[...], wo[:, pl.ds(low, cols)], preferred_element_type=f32)
        own[step] = share
        if step < 3:

            @pl.when(at_end)
            def _():
                part[step] = share.astype(jnp.bfloat16)
                for at in range(bands):
                    to_inner(step, at).start()

    def finish(at, terms):
        band = slice(at * piece, (at + 1) * piece)
        total = terms[0][band]
        for term in terms[1:]:
            total = total + term[band].astype(f32)
        final[band] = total.astype(jnp.bfloat16)
        hand(at).start()

    def add_on(index, at, mine, landed):
        band = slice(at * piece, (at + 1) * piece)
        part[index, band] = (mine[band] + landed[band].astype(f32)).astype(jnp.bfloat16)

    @pl.when(at_end)
    def _():
        for at in range(bands):
            to_end(at).wait_recv()
            finish(at, [own.at[3], from_inner.at[0]])
        for step in range(3):
            for at in range(bands):
                to_inner(step, at).wait_send()

    @pl.when(jnp.logical_not(at_end))
    def _():
        for at in range(bands):
            to_inner(0, at).wait_recv()
            add_on(0, at, own.at[0], from_outer.at[0])
            over_middle(0, at).start()
        for at in range(bands):
            to_inner(1, at).wait_recv()
            add_on(1, at, own.at[1], from_outer.at[1])
            over_middle(1, at).start()
            over_middle(0, at).wait_recv()
            add_on(2, at, own.at[3], from_inner.at[0])
            to_end(at).start()
        for at in range(bands):
            to_inner(2, at).wait_recv()
            over_middle(1, at).wait_recv()
            finish(at, [own.at[2], from_outer.at[2], from_inner.at[1]])
        for at in range(bands):
            over_middle(0, at).wait_send()
            over_middle(1, at).wait_send()
            to_end(at).wait_send()

    for group in range(groups):
        send_kv(0, 2, group, partner, 0).wait_send()
        send_kv(0, 1, group, partner, 1).wait_send()
        send_kv(2, 1, group, partner, 2).wait_send()
    for at in range(bands):
        hand(at).wait()


def solution(mesh):
    n_seg, n_ctx, n_tp = mesh.shape["segment"], mesh.shape["ctx"], mesh.shape["tp"]

    def body(hidden_in, norm_gain, query_weight, keyval_weight, output_weight, windows):
        rows, width = hidden_in.shape[1:]
        heads = query_weight.shape[2] // HD
        cols = output_weight.shape[2] // n_tp
        groups = keyval_weight.shape[2] // (2 * HD)
        bands = rows // PIECE
        half = HD // 2
        inverse = 10000.0 ** (-np.arange(half) / half)
        inverse = jnp.asarray(np.tile(inverse, 2)[None, :], dtype=jnp.float32)
        bf16 = jnp.bfloat16
        vmem = pl.BlockSpec(memory_space=pltpu.VMEM)
        hbm = pl.BlockSpec(memory_space=pl.ANY)
        return pl.pallas_call(
            functools.partial(block_kernel, n_seg, n_ctx, n_tp, PIECE),
            out_shape=pltpu.VMEM((1, rows, cols), bf16),
            in_specs=[pl.BlockSpec(memory_space=pltpu.SMEM)] + [hbm] * 6,
            out_specs=vmem,
            scratch_shapes=[
                pltpu.VMEM((1, width), bf16),
                pltpu.VMEM((1, HD), jnp.float32),
                pltpu.VMEM((rows, width), bf16),
                pltpu.VMEM(keyval_weight.shape[1:], bf16),
                pltpu.VMEM(query_weight.shape[1:], bf16),
                pltpu.VMEM(output_weight.shape[1:], bf16),
                pltpu.VMEM((rows, width), bf16),
                pltpu.VMEM((4, groups, rows, 2 * HD), bf16),
                pltpu.VMEM((heads, rows, HD), bf16),
                pltpu.VMEM((rows, heads * HD), bf16),
                pltpu.VMEM((4, rows, HD), jnp.float32),
                pltpu.VMEM((4, rows, cols), jnp.float32),
                pltpu.VMEM((3, rows, cols), bf16),
                pltpu.VMEM((3, rows, cols), bf16),
                pltpu.VMEM((2, rows, cols), bf16),
                pltpu.VMEM((rows, cols), bf16),
                pltpu.SemaphoreType.DMA((5 + DEPTHS,)),
                pltpu.SemaphoreType.DMA((3, groups)),
                pltpu.SemaphoreType.DMA((4, groups)),
                pltpu.SemaphoreType.DMA((3, bands)),
                pltpu.SemaphoreType.DMA((3, bands)),
                pltpu.SemaphoreType.DMA((2, bands)),
                pltpu.SemaphoreType.DMA((bands,)),
                pltpu.SemaphoreType.DMA((bands,)),
            ],
            compiler_params=pltpu.CompilerParams(
                collective_id=0, has_side_effects=True, vmem_limit_bytes=56 * 1024 * 1024
            ),
        )(
            windows,
            norm_gain,
            inverse,
            hidden_in,
            keyval_weight,
            query_weight,
            output_weight,
        )

    in_specs = (
        P("segment", "ctx", None),
        P("segment", None),
        P("segment", None, "tp"),
        P("segment", None, "tp"),
        P("segment", "tp", None),
        P("segment"),
    )
    out_specs = P("segment", "ctx", "tp")
    return jax.shard_map(body, mesh=mesh, in_specs=in_specs, out_specs=out_specs, check_vma=False)
```

```python
import functools

import jax
import jax.numpy as jnp
import numpy as np
from jax import lax
from jax.experimental import pallas as pl
from jax.experimental.pallas import tpu as pltpu
from jax.sharding import PartitionSpec as P

HD = 128
PIECE = 16
DEPTHS = 4
NORM_EPS = 1e-05
MESH = pl.DeviceIdType.MESH
LOG2E = 1.4426950408889634


def block_kernel(
    n_seg,
    n_ctx,
    n_tp,
    piece,
    win_ref,
    gain_hbm,
    inv_hbm,
    hid_hbm,
    wkv_hbm,
    wq_hbm,
    wo_hbm,
    out_ref,
    gain_row,
    inv_row,
    hid,
    wkv,
    wq,
    wo,
    normed,
    kv,
    query,
    probs,
    attn,
    bias,
    own,
    part,
    from_outer,
    from_inner,
    from_mate,
    from_behind,
    final,
    load_sem,
    kv_send,
    kv_recv,
    rs_send,
    outer_recv,
    inner_recv,
    mate_recv,
    z_send,
    z_recv,
):
    seg = lax.axis_index("segment")
    ctx = lax.axis_index("ctx")
    tp = lax.axis_index("tp")
    rows, width = hid.shape
    heads = query.shape[0]
    groups = kv.shape[1] // 2
    per_group = heads // groups
    cols = part.shape[2]

    depth = width // DEPTHS
    small = [
        pltpu.make_async_copy(inv_hbm, inv_row, load_sem.at[0]),
        pltpu.make_async_copy(gain_hbm, gain_row, load_sem.at[1]),
    ]
    load_hid = pltpu.make_async_copy(hid_hbm.at[0], hid, load_sem.at[2])
    load_wq = pltpu.make_async_copy(wq_hbm.at[0], wq, load_sem.at[3])
    load_wo = pltpu.make_async_copy(wo_hbm.at[0], wo, load_sem.at[4])
    load_wkv = []
    for at in range(DEPTHS):
        band = pl.ds(at * depth, depth)
        load_wkv.append(
            pltpu.make_async_copy(wkv_hbm.at[0, band], wkv.at[band], load_sem.at[5 + at])
        )
    for load in small + [load_hid] + load_wkv:
        load.start()

    def at_ctx(steps):
        return {"ctx": lax.rem(ctx + steps + n_ctx, n_ctx)}

    core = lax.rem(ctx, 2)
    partner = {"ctx": ctx + 1 - 2 * core}
    half = tp // 2
    inward = {"tp": tp + 1 - 2 * half}
    mate = tp + 1 - 2 * lax.rem(tp, 2)
    at_end = lax.rem(tp, 3) == 0

    barrier = pltpu.get_barrier_semaphore()
    peers = [partner]
    peers += [at_ctx(steps) for steps in (2, -2, 3, -3)]
    peers += [{"tp": lax.rem(tp + step, n_tp)} for step in range(1, n_tp)]
    peers += [
        {"segment": lax.rem(seg + 1, n_seg)},
        {"segment": lax.rem(seg + n_seg - 1, n_seg)},
        {"segment": lax.rem(seg + 1, n_seg), "tp": mate},
        {"segment": lax.rem(seg + n_seg - 1, n_seg), "tp": mate},
    ]
    for peer in peers:
        pl.semaphore_signal(barrier, inc=1, device_id=peer, device_id_type=MESH)

    small[0].wait()
    row_at = lax.broadcasted_iota(jnp.int32, (rows, HD), 0)
    lane_at = lax.broadcasted_iota(jnp.int32, (rows, HD), 1)
    angles = (ctx * rows + row_at).astype(jnp.float32) * inv_row[...]
    cosine = jnp.cos(angles)
    sine = jnp.sin(angles)
    sine = jnp.where(lane_at < HD // 2, -sine, sine)

    def rope(vector):
        return vector * cosine + pltpu.roll(vector, HD // 2, 1) * sine

    small[1].wait()
    load_hid.wait()
    gain = gain_row[...].astype(jnp.float32)
    for first in range(0, rows, 16):
        wide = hid[first : first + 16, :].astype(jnp.float32)
        scale = lax.rsqrt(jnp.sum(wide * wide, axis=1, keepdims=True) * (1.0 / width) + NORM_EPS)
        normed[first : first + 16, :] = (wide * scale * gain).astype(jnp.bfloat16)

    def send_kv(source, slot, group, target, sem):
        return pltpu.make_async_remote_copy(
            src_ref=kv.at[source, group],
            dst_ref=kv.at[slot, group],
            send_sem=kv_send.at[sem, group],
            recv_sem=kv_recv.at[slot, group],
            device_id=target,
            device_id_type=MESH,
        )

    both = None
    for at in range(DEPTHS):
        band = slice(at * depth, (at + 1) * depth)
        load_wkv[at].wait()
        term = jnp.dot(normed[:, band], wkv[band, :], preferred_element_type=jnp.float32)
        both = term if both is None else both + term
    for group in range(groups):
        low = group * 2 * HD
        kv[0, group] = rope(both[:, low : low + HD]).astype(jnp.bfloat16)
        kv[0, groups + group] = both[:, low + HD : low + 2 * HD].astype(jnp.bfloat16)
    pl.semaphore_wait(barrier, len(peers))
    for part_at in range(2 * groups):
        send_kv(0, 2, part_at, at_ctx(2), 0).start()

        @pl.when(core == 0)
        def _():
            send_kv(0, 1, part_at, partner, 1).start()

        @pl.when(core == 1)
        def _():
            send_kv(0, 3, part_at, at_ctx(3), 1).start()

    load_wq.start()
    load_wo.start()
    load_wq.wait()

    for pair in range(heads // 2):
        both = jnp.dot(
            normed[...],
            wq[:, pair * 2 * HD : (pair + 1) * 2 * HD],
            preferred_element_type=jnp.float32,
        )
        query[2 * pair] = rope(both[:, :HD]).astype(jnp.bfloat16)
        query[2 * pair + 1] = rope(both[:, HD:]).astype(jnp.bfloat16)

    window = win_ref[0]
    for slot in range(4):
        distance = row_at - lane_at + slot * rows
        inside = (distance >= 0) & (distance < window) & (ctx >= slot)
        bias[slot] = jnp.where(inside, jnp.float32(0.0), jnp.float32(-1e30))

    def pass_on(part_at):
        send_kv(0, 2, part_at, partner, 0).wait_recv()

        @pl.when(core == 0)
        def _():
            send_kv(2, 3, part_at, partner, 2).start()

        @pl.when(core == 1)
        def _():
            send_kv(2, 1, part_at, partner, 2).start()

    def here(part_at):
        send_kv(0, 1, part_at, partner, 1).wait_recv()
        send_kv(0, 3, part_at, partner, 2).wait_recv()

    def weigh(group):
        for head in range(group * per_group, (group + 1) * per_group):
            scores = []
            for slot in range(4):
                scores.append(
                    lax.dot_general(
                        query[head],
                        kv[slot, group],
                        (((1,), (1,)), ((), ())),
                        preferred_element_type=jnp.float32,
                    )
                    + bias[slot]
                )
            highest = jnp.max(
                jnp.maximum(
                    jnp.maximum(scores[0], scores[1]), jnp.maximum(scores[2], scores[3])
                ),
                axis=1,
                keepdims=True,
            )
            expo = [jnp.exp2((score - highest) * (HD**-0.5 * LOG2E)) for score in scores]
            total = jnp.sum((expo[0] + expo[1]) + (expo[2] + expo[3]), axis=1, keepdims=True)
            inverse = 1.0 / total
            for slot in range(4):
                probs[head, slot] = (expo[slot] * inverse).astype(jnp.bfloat16)

    def mix(group):
        for head in range(group * per_group, (group + 1) * per_group):
            mixed = None
            for slot in range(4):
                term = jnp.dot(
                    probs[head, slot], kv[slot, groups + group], preferred_element_type=jnp.float32
                )
                mixed = term if mixed is None else mixed + term
            attn[:, head * HD : (head + 1) * HD] = mixed.astype(jnp.bfloat16)

    for part_at in range(groups):
        pass_on(part_at)
    for group in range(groups):
        here(group)
        weigh(group)
        pass_on(groups + group)
    for group in range(groups):
        here(groups + group)
        mix(group)

    load_wo.wait()

    bands = rows // piece
    ahead_too = seg == n_seg - 1
    from_last = seg == 0

    def send_part(index, at, place, sem, target):
        band = pl.ds(at * piece, piece)
        return pltpu.make_async_remote_copy(
            src_ref=part.at[index, band],
            dst_ref=place.at[band],
            send_sem=rs_send.at[index, at],
            recv_sem=sem.at[at],
            device_id=target,
            device_id_type=MESH,
        )

    def to_inner(index, at):
        return send_part(index, at, from_outer.at[index], outer_recv.at[index], inward)

    def over_middle(index, at):
        return send_part(index, at, from_inner.at[index], inner_recv.at[index], inward)

    def to_end(at):
        outward = {"tp": tp - 1 + 2 * half}
        return send_part(2, at, from_inner.at[0], inner_recv.at[0], outward)

    def skip_ahead(at):
        return pltpu.make_async_remote_copy(
            src_ref=part.at[2, pl.ds(at * piece, piece)],
            dst_ref=from_mate.at[at],
            send_sem=rs_send.at[2, at],
            recv_sem=mate_recv.at[at],
            device_id={"segment": lax.rem(seg + 1, n_seg), "tp": mate},
            device_id_type=MESH,
        )

    def rest_ahead(at):
        return pltpu.make_async_remote_copy(
            src_ref=final.at[pl.ds(at * piece, piece)],
            dst_ref=from_behind.at[at],
            send_sem=z_send.at[at],
            recv_sem=z_recv.at[at],
            device_id={"segment": lax.rem(seg + 1, n_seg)},
            device_id_type=MESH,
        )

    def hand(at):
        band = pl.ds(at * piece, piece)
        return pltpu.make_async_remote_copy(
            src_ref=final.at[band],
            dst_ref=out_ref.at[0, band],
            send_sem=z_send.at[at],
            recv_sem=z_recv.at[at],
            device_id={"segment": lax.rem(seg + 1, n_seg)},
            device_id_type=MESH,
        )

    f32 = jnp.float32
    for step in range(4):
        mirrored = 3 - step
        low = pl.multiple_of((mirrored + half * (3 - 2 * mirrored)) * cols, cols)
        share = jnp.dot(attn[...], wo[:, pl.ds(low, cols)], preferred_element_type=f32)
        own[step] = share
        if step < 3:

            @pl.when(at_end)
            def _():
                part[step] = share.astype(jnp.bfloat16)
                if step < 2:
                    for at in range(bands):
                        to_inner(step, at).start()
                else:

                    @pl.when(ahead_too)
                    def _():
                        for at in range(bands):
                            skip_ahead(at).start()

                    @pl.when(jnp.logical_not(ahead_too))
                    def _():
                        for at in range(bands):
                            to_inner(2, at).start()

    def finish(at, terms):
        band = slice(at * piece, (at + 1) * piece)
        total = terms[0][band]
        for term in terms[1:]:
            total = total + term[band].astype(f32)
        final[band] = total.astype(jnp.bfloat16)
        hand(at).start()

    def add_on(index, at, mine, landed):
        band = slice(at * piece, (at + 1) * piece)
        part[index, band] = (mine[band] + landed[band].astype(f32)).astype(jnp.bfloat16)

    @pl.when(at_end)
    def _():
        for at in range(bands):
            to_end(at).wait_recv()
            finish(at, [own.at[3], from_inner.at[0]])
        for step in range(3):
            for at in range(bands):
                to_inner(step, at).wait_send()
        for at in range(bands):
            hand(at).wait()

    @pl.when(jnp.logical_not(at_end))
    def _():
        for at in range(bands):
            to_inner(0, at).wait_recv()
            add_on(0, at, own.at[0], from_outer.at[0])
            over_middle(0, at).start()
        for at in range(bands):
            to_inner(1, at).wait_recv()
            add_on(1, at, own.at[1], from_outer.at[1])
            over_middle(1, at).start()
            over_middle(0, at).wait_recv()
            add_on(2, at, own.at[3], from_inner.at[0])
            to_end(at).start()

        @pl.when(ahead_too)
        def _():
            for at in range(bands):
                over_middle(1, at).wait_recv()
                band = slice(at * piece, (at + 1) * piece)
                rest = own[2, band] + from_inner[1, band].astype(f32)
                final[band] = rest.astype(jnp.bfloat16)
                rest_ahead(at).start()

        @pl.when(jnp.logical_not(ahead_too))
        def _():
            for at in range(bands):
                to_inner(2, at).wait_recv()
                over_middle(1, at).wait_recv()
                finish(at, [own.at[2], from_outer.at[2], from_inner.at[1]])

        for at in range(bands):
            over_middle(0, at).wait_send()
            over_middle(1, at).wait_send()
            to_end(at).wait_send()
        for at in range(bands):
            hand(at).wait_send()

        @pl.when(from_last)
        def _():
            for at in range(bands):
                rest_ahead(at).wait_recv()
                skip_ahead(at).wait_recv()
                band = slice(at * piece, (at + 1) * piece)
                total = from_behind[at].astype(f32) + from_mate[at].astype(f32)
                out_ref[0, band] = total.astype(jnp.bfloat16)

        @pl.when(jnp.logical_not(from_last))
        def _():
            for at in range(bands):
                hand(at).wait_recv()

    for part_at in range(2 * groups):
        send_kv(0, 2, part_at, partner, 0).wait_send()
        send_kv(0, 1, part_at, partner, 1).wait_send()
        send_kv(2, 1, part_at, partner, 2).wait_send()


def solution(mesh):
    n_seg, n_ctx, n_tp = mesh.shape["segment"], mesh.shape["ctx"], mesh.shape["tp"]

    def body(hidden_in, norm_gain, query_weight, keyval_weight, output_weight, windows):
        rows, width = hidden_in.shape[1:]
        heads = query_weight.shape[2] // HD
        cols = output_weight.shape[2] // n_tp
        groups = keyval_weight.shape[2] // (2 * HD)
        bands = rows // PIECE
        half = HD // 2
        inverse = 10000.0 ** (-np.arange(half) / half)
        inverse = jnp.asarray(np.tile(inverse, 2)[None, :], dtype=jnp.float32)
        bf16 = jnp.bfloat16
        vmem = pl.BlockSpec(memory_space=pltpu.VMEM)
        hbm = pl.BlockSpec(memory_space=pl.ANY)
        return pl.pallas_call(
            functools.partial(block_kernel, n_seg, n_ctx, n_tp, PIECE),
            out_shape=pltpu.VMEM((1, rows, cols), bf16),
            in_specs=[pl.BlockSpec(memory_space=pltpu.SMEM)] + [hbm] * 6,
            out_specs=vmem,
            scratch_shapes=[
                pltpu.VMEM((1, width), bf16),
                pltpu.VMEM((1, HD), jnp.float32),
                pltpu.VMEM((rows, width), bf16),
                pltpu.VMEM(keyval_weight.shape[1:], bf16),
                pltpu.VMEM(query_weight.shape[1:], bf16),
                pltpu.VMEM(output_weight.shape[1:], bf16),
                pltpu.VMEM((rows, width), bf16),
                pltpu.VMEM((4, 2 * groups, rows, HD), bf16),
                pltpu.VMEM((heads, rows, HD), bf16),
                pltpu.VMEM((heads, 4, rows, HD), bf16),
                pltpu.VMEM((rows, heads * HD), bf16),
                pltpu.VMEM((4, rows, HD), jnp.float32),
                pltpu.VMEM((4, rows, cols), jnp.float32),
                pltpu.VMEM((3, rows, cols), bf16),
                pltpu.VMEM((3, rows, cols), bf16),
                pltpu.VMEM((2, rows, cols), bf16),
                pltpu.VMEM((bands, PIECE, cols), bf16),
                pltpu.VMEM((bands, PIECE, cols), bf16),
                pltpu.VMEM((rows, cols), bf16),
                pltpu.SemaphoreType.DMA((5 + DEPTHS,)),
                pltpu.SemaphoreType.DMA((3, 2 * groups)),
                pltpu.SemaphoreType.DMA((4, 2 * groups)),
                pltpu.SemaphoreType.DMA((3, bands)),
                pltpu.SemaphoreType.DMA((3, bands)),
                pltpu.SemaphoreType.DMA((2, bands)),
                pltpu.SemaphoreType.DMA((bands,)),
                pltpu.SemaphoreType.DMA((bands,)),
                pltpu.SemaphoreType.DMA((bands,)),
            ],
            compiler_params=pltpu.CompilerParams(
                collective_id=0, has_side_effects=True, vmem_limit_bytes=56 * 1024 * 1024
            ),
        )(
            windows,
            norm_gain,
            inverse,
            hidden_in,
            keyval_weight,
            query_weight,
            output_weight,
        )

    in_specs = (
        P("segment", "ctx", None),
        P("segment", None),
        P("segment", None, "tp"),
        P("segment", None, "tp"),
        P("segment", "tp", None),
        P("segment"),
    )
    out_specs = P("segment", "ctx", "tp")
    return jax.shard_map(body, mesh=mesh, in_specs=in_specs, out_specs=out_specs, check_vma=False)
```

```python
import functools

import jax
import jax.numpy as jnp
import numpy as np
from jax import lax
from jax.experimental import pallas as pl
from jax.experimental.pallas import tpu as pltpu
from jax.sharding import PartitionSpec as P

HD = 128
PIECE = 16
DEPTHS = 4
NORM_EPS = 1e-05
MESH = pl.DeviceIdType.MESH
LOG2E = 1.4426950408889634


def block_kernel(
    n_seg,
    n_ctx,
    n_tp,
    piece,
    win_ref,
    gain_hbm,
    inv_hbm,
    hid_hbm,
    wkv_hbm,
    wq_hbm,
    wo_hbm,
    out_ref,
    gain_row,
    inv_row,
    hid,
    wkv,
    wq,
    wo,
    normed,
    kv,
    query,
    probs,
    attn,
    bias,
    own,
    part,
    from_outer,
    from_inner,
    from_mate,
    from_behind,
    final,
    load_sem,
    kv_send,
    kv_recv,
    rs_send,
    outer_recv,
    inner_recv,
    mate_recv,
    z_send,
    z_recv,
):
    seg = lax.axis_index("segment")
    ctx = lax.axis_index("ctx")
    tp = lax.axis_index("tp")
    rows, width = hid.shape
    heads = query.shape[0]
    groups = kv.shape[1] // 2
    per_group = heads // groups
    cols = part.shape[2]

    depth = width // DEPTHS
    small = [
        pltpu.make_async_copy(inv_hbm, inv_row, load_sem.at[0]),
        pltpu.make_async_copy(gain_hbm, gain_row, load_sem.at[1]),
    ]
    load_hid = pltpu.make_async_copy(hid_hbm.at[0], hid, load_sem.at[2])
    load_wq = pltpu.make_async_copy(wq_hbm.at[0], wq, load_sem.at[3])
    load_wo = pltpu.make_async_copy(wo_hbm.at[0], wo, load_sem.at[4])
    load_wkv = []
    for at in range(DEPTHS):
        band = pl.ds(at * depth, depth)
        load_wkv.append(
            pltpu.make_async_copy(wkv_hbm.at[0, band], wkv.at[band], load_sem.at[5 + at])
        )
    for load in small + [load_hid] + load_wkv:
        load.start()

    def at_ctx(steps):
        return {"ctx": lax.rem(ctx + steps + n_ctx, n_ctx)}

    core = lax.rem(ctx, 2)
    partner = {"ctx": ctx + 1 - 2 * core}
    half = tp // 2
    inward = {"tp": tp + 1 - 2 * half}
    mate = tp + 1 - 2 * lax.rem(tp, 2)
    at_end = lax.rem(tp, 3) == 0

    barrier = pltpu.get_barrier_semaphore()
    behind = lax.rem(seg + n_seg - 1, n_seg)
    peers = [partner, at_ctx(-2), at_ctx(-3)]
    peers += [{"tp": mate}, {"tp": n_tp - 1 - tp}]
    peers += [{"segment": behind}, {"segment": behind, "tp": mate}]
    for peer in peers:
        pl.semaphore_signal(barrier, inc=1, device_id=peer, device_id_type=MESH)

    small[0].wait()
    row_at = lax.broadcasted_iota(jnp.int32, (rows, HD), 0)
    lane_at = lax.broadcasted_iota(jnp.int32, (rows, HD), 1)
    angles = (ctx * rows + row_at).astype(jnp.float32) * inv_row[...]
    cosine = jnp.cos(angles)
    sine = jnp.sin(angles)
    sine = jnp.where(lane_at < HD // 2, -sine, sine)

    def rope(vector):
        return vector * cosine + pltpu.roll(vector, HD // 2, 1) * sine

    small[1].wait()
    load_hid.wait()
    gain = gain_row[...].astype(jnp.float32)
    for first in range(0, rows, 16):
        wide = hid[first : first + 16, :].astype(jnp.float32)
        scale = lax.rsqrt(jnp.sum(wide * wide, axis=1, keepdims=True) * (1.0 / width) + NORM_EPS)
        normed[first : first + 16, :] = (wide * scale * gain).astype(jnp.bfloat16)

    def send_kv(source, slot, group, target, sem):
        return pltpu.make_async_remote_copy(
            src_ref=kv.at[source, group],
            dst_ref=kv.at[slot, group],
            send_sem=kv_send.at[sem, group],
            recv_sem=kv_recv.at[slot, group],
            device_id=target,
            device_id_type=MESH,
        )

    both = None
    for at in range(DEPTHS):
        band = slice(at * depth, (at + 1) * depth)
        load_wkv[at].wait()
        term = jnp.dot(normed[:, band], wkv[band, :], preferred_element_type=jnp.float32)
        both = term if both is None else both + term
    for group in range(groups):
        low = group * 2 * HD
        kv[0, group] = rope(both[:, low : low + HD]).astype(jnp.bfloat16)
        kv[0, groups + group] = both[:, low + HD : low + 2 * HD].astype(jnp.bfloat16)
    pl.semaphore_wait(barrier, len(peers))
    for part_at in range(2 * groups):
        send_kv(0, 2, part_at, at_ctx(2), 0).start()

        @pl.when(core == 0)
        def _():
            send_kv(0, 1, part_at, partner, 1).start()

        @pl.when(core == 1)
        def _():
            send_kv(0, 3, part_at, at_ctx(3), 1).start()

    load_wq.start()
    load_wo.start()
    load_wq.wait()

    for pair in range(heads // 2):
        both = jnp.dot(
            normed[...],
            wq[:, pair * 2 * HD : (pair + 1) * 2 * HD],
            preferred_element_type=jnp.float32,
        )
        query[2 * pair] = rope(both[:, :HD]).astype(jnp.bfloat16)
        query[2 * pair + 1] = rope(both[:, HD:]).astype(jnp.bfloat16)

    window = win_ref[0]
    for slot in range(4):
        distance = row_at - lane_at + slot * rows
        inside = (distance >= 0) & (distance < window) & (ctx >= slot)
        bias[slot] = jnp.where(inside, jnp.float32(0.0), jnp.float32(-1e30))

    def pass_on(part_at):
        send_kv(0, 2, part_at, partner, 0).wait_recv()

        @pl.when(core == 0)
        def _():
            send_kv(2, 3, part_at, partner, 2).start()

        @pl.when(core == 1)
        def _():
            send_kv(2, 1, part_at, partner, 2).start()

    def here(part_at):
        send_kv(0, 1, part_at, partner, 1).wait_recv()
        send_kv(0, 3, part_at, partner, 2).wait_recv()

    def weigh(group):
        for head in range(group * per_group, (group + 1) * per_group):
            scores = []
            for slot in range(4):
                scores.append(
                    lax.dot_general(
                        query[head],
                        kv[slot, group],
                        (((1,), (1,)), ((), ())),
                        preferred_element_type=jnp.float32,
                    )
                    + bias[slot]
                )
            highest = jnp.max(
                jnp.maximum(
                    jnp.maximum(scores[0], scores[1]), jnp.maximum(scores[2], scores[3])
                ),
                axis=1,
                keepdims=True,
            )
            expo = [jnp.exp2((score - highest) * (HD**-0.5 * LOG2E)) for score in scores]
            total = jnp.sum((expo[0] + expo[1]) + (expo[2] + expo[3]), axis=1, keepdims=True)
            inverse = 1.0 / total
            for slot in range(4):
                probs[head, slot] = (expo[slot] * inverse).astype(jnp.bfloat16)

    def mix(group):
        for head in range(group * per_group, (group + 1) * per_group):
            mixed = None
            for slot in range(4):
                term = jnp.dot(
                    probs[head, slot], kv[slot, groups + group], preferred_element_type=jnp.float32
                )
                mixed = term if mixed is None else mixed + term
            attn[:, head * HD : (head + 1) * HD] = mixed.astype(jnp.bfloat16)

    for part_at in range(groups):
        pass_on(part_at)
    for group in range(groups):
        here(group)
        weigh(group)
        pass_on(groups + group)
    for group in range(groups):
        here(groups + group)
        mix(group)

    load_wo.wait()

    bands = rows // piece
    ahead_too = seg == n_seg - 1
    from_last = seg == 0

    def send_part(index, at, place, sem, target):
        band = pl.ds(at * piece, piece)
        return pltpu.make_async_remote_copy(
            src_ref=part.at[index, band],
            dst_ref=place.at[band],
            send_sem=rs_send.at[index, at],
            recv_sem=sem.at[at],
            device_id=target,
            device_id_type=MESH,
        )

    def to_inner(index, at):
        return send_part(index, at, from_outer.at[index], outer_recv.at[index], inward)

    def over_middle(index, at):
        return send_part(index, at, from_inner.at[index], inner_recv.at[index], inward)

    def to_end(at):
        outward = {"tp": tp - 1 + 2 * half}
        return send_part(2, at, from_inner.at[0], inner_recv.at[0], outward)

    def skip_ahead(at):
        return pltpu.make_async_remote_copy(
            src_ref=part.at[2, pl.ds(at * piece, piece)],
            dst_ref=from_mate.at[at],
            send_sem=rs_send.at[2, at],
            recv_sem=mate_recv.at[at],
            device_id={"segment": lax.rem(seg + 1, n_seg), "tp": mate},
            device_id_type=MESH,
        )

    def rest_ahead(at):
        return pltpu.make_async_remote_copy(
            src_ref=final.at[pl.ds(at * piece, piece)],
            dst_ref=from_behind.at[at],
            send_sem=z_send.at[at],
            recv_sem=z_recv.at[at],
            device_id={"segment": lax.rem(seg + 1, n_seg)},
            device_id_type=MESH,
        )

    def hand(at):
        band = pl.ds(at * piece, piece)
        return pltpu.make_async_remote_copy(
            src_ref=final.at[band],
            dst_ref=out_ref.at[0, band],
            send_sem=z_send.at[at],
            recv_sem=z_recv.at[at],
            device_id={"segment": lax.rem(seg + 1, n_seg)},
            device_id_type=MESH,
        )

    f32 = jnp.float32
    for step in range(4):
        mirrored = 3 - step
        low = pl.multiple_of((mirrored + half * (3 - 2 * mirrored)) * cols, cols)
        share = jnp.dot(attn[...], wo[:, pl.ds(low, cols)], preferred_element_type=f32)
        own[step] = share
        if step < 3:

            @pl.when(at_end)
            def _():
                part[step] = share.astype(jnp.bfloat16)
                if step < 2:
                    for at in range(bands):
                        to_inner(step, at).start()
                else:

                    @pl.when(ahead_too)
                    def _():
                        for at in range(bands):
                            skip_ahead(at).start()

                    @pl.when(jnp.logical_not(ahead_too))
                    def _():
                        for at in range(bands):
                            to_inner(2, at).start()

    def finish(at, terms):
        band = slice(at * piece, (at + 1) * piece)
        total = terms[0][band]
        for term in terms[1:]:
            total = total + term[band].astype(f32)
        final[band] = total.astype(jnp.bfloat16)
        hand(at).start()

    def add_on(index, at, mine, landed):
        band = slice(at * piece, (at + 1) * piece)
        part[index, band] = (mine[band] + landed[band].astype(f32)).astype(jnp.bfloat16)

    @pl.when(at_end)
    def _():
        for at in range(bands):
            to_end(at).wait_recv()
            finish(at, [own.at[3], from_inner.at[0]])
        for step in range(3):
            for at in range(bands):
                to_inner(step, at).wait_send()
        for at in range(bands):
            hand(at).wait()

    @pl.when(jnp.logical_not(at_end))
    def _():
        for at in range(bands):
            to_inner(0, at).wait_recv()
            add_on(0, at, own.at[0], from_outer.at[0])
            over_middle(0, at).start()
        for at in range(bands):
            over_middle(0, at).wait_recv()
            add_on(2, at, own.at[3], from_inner.at[0])
            to_end(at).start()
            to_inner(1, at).wait_recv()
            add_on(1, at, own.at[1], from_outer.at[1])
            over_middle(1, at).start()

        @pl.when(ahead_too)
        def _():
            for at in range(bands):
                over_middle(1, at).wait_recv()
                band = slice(at * piece, (at + 1) * piece)
                rest = own[2, band] + from_inner[1, band].astype(f32)
                final[band] = rest.astype(jnp.bfloat16)
                rest_ahead(at).start()

        @pl.when(jnp.logical_not(ahead_too))
        def _():
            for at in range(bands):
                to_inner(2, at).wait_recv()
                over_middle(1, at).wait_recv()
                finish(at, [own.at[2], from_outer.at[2], from_inner.at[1]])

        for at in range(bands):
            over_middle(0, at).wait_send()
            over_middle(1, at).wait_send()
            to_end(at).wait_send()
        for at in range(bands):
            hand(at).wait_send()

        @pl.when(from_last)
        def _():
            for at in range(bands):
                rest_ahead(at).wait_recv()
                skip_ahead(at).wait_recv()
                band = slice(at * piece, (at + 1) * piece)
                total = from_behind[at].astype(f32) + from_mate[at].astype(f32)
                out_ref[0, band] = total.astype(jnp.bfloat16)

        @pl.when(jnp.logical_not(from_last))
        def _():
            for at in range(bands):
                hand(at).wait_recv()

    for part_at in range(2 * groups):
        send_kv(0, 2, part_at, partner, 0).wait_send()
        send_kv(0, 1, part_at, partner, 1).wait_send()
        send_kv(2, 1, part_at, partner, 2).wait_send()


def solution(mesh):
    n_seg, n_ctx, n_tp = mesh.shape["segment"], mesh.shape["ctx"], mesh.shape["tp"]

    def body(hidden_in, norm_gain, query_weight, keyval_weight, output_weight, windows):
        rows, width = hidden_in.shape[1:]
        heads = query_weight.shape[2] // HD
        cols = output_weight.shape[2] // n_tp
        groups = keyval_weight.shape[2] // (2 * HD)
        bands = rows // PIECE
        half = HD // 2
        inverse = 10000.0 ** (-np.arange(half) / half)
        inverse = jnp.asarray(np.tile(inverse, 2)[None, :], dtype=jnp.float32)
        bf16 = jnp.bfloat16
        vmem = pl.BlockSpec(memory_space=pltpu.VMEM)
        hbm = pl.BlockSpec(memory_space=pl.ANY)
        return pl.pallas_call(
            functools.partial(block_kernel, n_seg, n_ctx, n_tp, PIECE),
            out_shape=pltpu.VMEM((1, rows, cols), bf16),
            in_specs=[pl.BlockSpec(memory_space=pltpu.SMEM)] + [hbm] * 6,
            out_specs=vmem,
            scratch_shapes=[
                pltpu.VMEM((1, width), bf16),
                pltpu.VMEM((1, HD), jnp.float32),
                pltpu.VMEM((rows, width), bf16),
                pltpu.VMEM(keyval_weight.shape[1:], bf16),
                pltpu.VMEM(query_weight.shape[1:], bf16),
                pltpu.VMEM(output_weight.shape[1:], bf16),
                pltpu.VMEM((rows, width), bf16),
                pltpu.VMEM((4, 2 * groups, rows, HD), bf16),
                pltpu.VMEM((heads, rows, HD), bf16),
                pltpu.VMEM((heads, 4, rows, HD), bf16),
                pltpu.VMEM((rows, heads * HD), bf16),
                pltpu.VMEM((4, rows, HD), jnp.float32),
                pltpu.VMEM((4, rows, cols), jnp.float32),
                pltpu.VMEM((3, rows, cols), bf16),
                pltpu.VMEM((3, rows, cols), bf16),
                pltpu.VMEM((2, rows, cols), bf16),
                pltpu.VMEM((bands, PIECE, cols), bf16),
                pltpu.VMEM((bands, PIECE, cols), bf16),
                pltpu.VMEM((rows, cols), bf16),
                pltpu.SemaphoreType.DMA((5 + DEPTHS,)),
                pltpu.SemaphoreType.DMA((3, 2 * groups)),
                pltpu.SemaphoreType.DMA((4, 2 * groups)),
                pltpu.SemaphoreType.DMA((3, bands)),
                pltpu.SemaphoreType.DMA((3, bands)),
                pltpu.SemaphoreType.DMA((2, bands)),
                pltpu.SemaphoreType.DMA((bands,)),
                pltpu.SemaphoreType.DMA((bands,)),
                pltpu.SemaphoreType.DMA((bands,)),
            ],
            compiler_params=pltpu.CompilerParams(
                collective_id=0, has_side_effects=True, vmem_limit_bytes=56 * 1024 * 1024
            ),
        )(
            windows,
            norm_gain,
            inverse,
            hidden_in,
            keyval_weight,
            query_weight,
            output_weight,
        )

    in_specs = (
        P("segment", "ctx", None),
        P("segment", None),
        P("segment", None, "tp"),
        P("segment", None, "tp"),
        P("segment", "tp", None),
        P("segment"),
    )
    out_specs = P("segment", "ctx", "tp")
    return jax.shard_map(body, mesh=mesh, in_specs=in_specs, out_specs=out_specs, check_vma=False)
```

```python
import functools

import jax
import jax.numpy as jnp
import numpy as np
from jax import lax
from jax.experimental import pallas as pl
from jax.experimental.pallas import tpu as pltpu
from jax.sharding import PartitionSpec as P

HD = 128
PIECE = 16
DEPTHS = 4
FAR = 3
NORM_EPS = 1e-05
MESH = pl.DeviceIdType.MESH
LOG2E = 1.4426950408889634


def block_kernel(
    n_seg,
    n_ctx,
    n_tp,
    piece,
    win_ref,
    gain_hbm,
    inv_hbm,
    hid_hbm,
    wkv_hbm,
    wq_hbm,
    wo_hbm,
    out_ref,
    gain_row,
    inv_row,
    hid,
    wkv,
    wq,
    wo,
    normed,
    kv,
    query,
    probs,
    attn,
    bias,
    own,
    part,
    from_outer,
    from_inner,
    from_far,
    from_mate,
    from_behind,
    final,
    load_sem,
    kv_send,
    kv_recv,
    rs_send,
    outer_recv,
    inner_recv,
    far_recv,
    mate_recv,
    z_send,
    z_recv,
):
    seg = lax.axis_index("segment")
    ctx = lax.axis_index("ctx")
    tp = lax.axis_index("tp")
    rows, width = hid.shape
    heads = query.shape[0]
    groups = kv.shape[1] // 2
    per_group = heads // groups
    cols = part.shape[2]

    depth = width // DEPTHS
    small = [
        pltpu.make_async_copy(inv_hbm, inv_row, load_sem.at[0]),
        pltpu.make_async_copy(gain_hbm, gain_row, load_sem.at[1]),
    ]
    load_hid = pltpu.make_async_copy(hid_hbm.at[0], hid, load_sem.at[2])
    load_wq = pltpu.make_async_copy(wq_hbm.at[0], wq, load_sem.at[3])
    load_wo = pltpu.make_async_copy(wo_hbm.at[0], wo, load_sem.at[4])
    load_wkv = []
    for at in range(DEPTHS):
        band = pl.ds(at * depth, depth)
        load_wkv.append(
            pltpu.make_async_copy(wkv_hbm.at[0, band], wkv.at[band], load_sem.at[5 + at])
        )
    for load in small + [load_hid] + load_wkv:
        load.start()

    def at_ctx(steps):
        return {"ctx": lax.rem(ctx + steps + n_ctx, n_ctx)}

    core = lax.rem(ctx, 2)
    partner = {"ctx": ctx + 1 - 2 * core}
    half = tp // 2
    inward = {"tp": tp + 1 - 2 * half}
    mate = tp + 1 - 2 * lax.rem(tp, 2)
    at_end = lax.rem(tp, 3) == 0

    barrier = pltpu.get_barrier_semaphore()
    behind = lax.rem(seg + n_seg - 1, n_seg)
    peers = [partner, at_ctx(-2), at_ctx(-3)]
    peers += [{"tp": mate}, {"tp": n_tp - 1 - tp}]
    across_two = lax.rem(tp + 2, n_tp)
    peers += [{"segment": behind, "tp": other} for other in (tp, mate, across_two)]
    for peer in peers:
        pl.semaphore_signal(barrier, inc=1, device_id=peer, device_id_type=MESH)

    small[0].wait()
    row_at = lax.broadcasted_iota(jnp.int32, (rows, HD), 0)
    lane_at = lax.broadcasted_iota(jnp.int32, (rows, HD), 1)
    angles = (ctx * rows + row_at).astype(jnp.float32) * inv_row[...]
    cosine = jnp.cos(angles)
    sine = jnp.sin(angles)
    sine = jnp.where(lane_at < HD // 2, -sine, sine)

    def rope(vector):
        return vector * cosine + pltpu.roll(vector, HD // 2, 1) * sine

    small[1].wait()
    load_hid.wait()
    gain = gain_row[...].astype(jnp.float32)
    for first in range(0, rows, 16):
        wide = hid[first : first + 16, :].astype(jnp.float32)
        scale = lax.rsqrt(jnp.sum(wide * wide, axis=1, keepdims=True) * (1.0 / width) + NORM_EPS)
        normed[first : first + 16, :] = (wide * scale * gain).astype(jnp.bfloat16)

    def send_kv(source, slot, group, target, sem):
        return pltpu.make_async_remote_copy(
            src_ref=kv.at[source, group],
            dst_ref=kv.at[slot, group],
            send_sem=kv_send.at[sem, group],
            recv_sem=kv_recv.at[slot, group],
            device_id=target,
            device_id_type=MESH,
        )

    both = None
    for at in range(DEPTHS):
        band = slice(at * depth, (at + 1) * depth)
        load_wkv[at].wait()
        term = jnp.dot(normed[:, band], wkv[band, :], preferred_element_type=jnp.float32)
        both = term if both is None else both + term
    for group in range(groups):
        low = group * 2 * HD
        kv[0, group] = rope(both[:, low : low + HD]).astype(jnp.bfloat16)
        kv[0, groups + group] = both[:, low + HD : low + 2 * HD].astype(jnp.bfloat16)
    pl.semaphore_wait(barrier, len(peers))
    for part_at in range(2 * groups):
        send_kv(0, 2, part_at, at_ctx(2), 0).start()

        @pl.when(core == 0)
        def _():
            send_kv(0, 1, part_at, partner, 1).start()

        @pl.when(core == 1)
        def _():
            send_kv(0, 3, part_at, at_ctx(3), 1).start()

    load_wq.start()
    load_wo.start()
    load_wq.wait()

    for pair in range(heads // 2):
        both = jnp.dot(
            normed[...],
            wq[:, pair * 2 * HD : (pair + 1) * 2 * HD],
            preferred_element_type=jnp.float32,
        )
        query[2 * pair] = rope(both[:, :HD]).astype(jnp.bfloat16)
        query[2 * pair + 1] = rope(both[:, HD:]).astype(jnp.bfloat16)

    window = win_ref[0]
    for slot in range(4):
        distance = row_at - lane_at + slot * rows
        inside = (distance >= 0) & (distance < window) & (ctx >= slot)
        bias[slot] = jnp.where(inside, jnp.float32(0.0), jnp.float32(-1e30))

    def pass_on(part_at):
        send_kv(0, 2, part_at, partner, 0).wait_recv()

        @pl.when(core == 0)
        def _():
            send_kv(2, 3, part_at, partner, 2).start()

        @pl.when(core == 1)
        def _():
            send_kv(2, 1, part_at, partner, 2).start()

    def here(part_at):
        send_kv(0, 1, part_at, partner, 1).wait_recv()
        send_kv(0, 3, part_at, partner, 2).wait_recv()

    def weigh(group):
        for head in range(group * per_group, (group + 1) * per_group):
            scores = []
            for slot in range(4):
                scores.append(
                    lax.dot_general(
                        query[head],
                        kv[slot, group],
                        (((1,), (1,)), ((), ())),
                        preferred_element_type=jnp.float32,
                    )
                    + bias[slot]
                )
            highest = jnp.max(
                jnp.maximum(
                    jnp.maximum(scores[0], scores[1]), jnp.maximum(scores[2], scores[3])
                ),
                axis=1,
                keepdims=True,
            )
            expo = [jnp.exp2((score - highest) * (HD**-0.5 * LOG2E)) for score in scores]
            total = jnp.sum((expo[0] + expo[1]) + (expo[2] + expo[3]), axis=1, keepdims=True)
            inverse = 1.0 / total
            for slot in range(4):
                probs[head, slot] = (expo[slot] * inverse).astype(jnp.bfloat16)

    def mix(group):
        for head in range(group * per_group, (group + 1) * per_group):
            mixed = None
            for slot in range(4):
                term = jnp.dot(
                    probs[head, slot], kv[slot, groups + group], preferred_element_type=jnp.float32
                )
                mixed = term if mixed is None else mixed + term
            attn[:, head * HD : (head + 1) * HD] = mixed.astype(jnp.bfloat16)

    for part_at in range(groups):
        pass_on(part_at)
    for group in range(groups):
        here(group)
        weigh(group)
        pass_on(groups + group)
    for group in range(groups):
        here(groups + group)
        mix(group)

    load_wo.wait()

    bands = rows // piece
    near = bands - FAR
    ahead_too = seg == n_seg - 1
    from_last = seg == 0

    def send_part(index, at, place, sem, target):
        band = pl.ds(at * piece, piece)
        return pltpu.make_async_remote_copy(
            src_ref=part.at[index, band],
            dst_ref=place.at[band],
            send_sem=rs_send.at[index, at],
            recv_sem=sem.at[at],
            device_id=target,
            device_id_type=MESH,
        )

    def to_inner(index, at):
        return send_part(index, at, from_outer.at[index], outer_recv.at[index], inward)

    def over_middle(index, at):
        return send_part(index, at, from_inner.at[index], inner_recv.at[index], inward)

    def to_end(at):
        outward = {"tp": tp - 1 + 2 * half}
        return send_part(2, at, from_inner.at[0], inner_recv.at[0], outward)

    def skip_ahead(at):
        return pltpu.make_async_remote_copy(
            src_ref=part.at[2, pl.ds(at * piece, piece)],
            dst_ref=from_mate.at[at],
            send_sem=rs_send.at[2, at],
            recv_sem=mate_recv.at[at],
            device_id={"segment": lax.rem(seg + 1, n_seg), "tp": mate},
            device_id_type=MESH,
        )

    def skip_far(at):
        return pltpu.make_async_remote_copy(
            src_ref=part.at[1, pl.ds(at * piece, piece)],
            dst_ref=from_far.at[at - near],
            send_sem=rs_send.at[1, at],
            recv_sem=far_recv.at[at - near],
            device_id={"segment": lax.rem(seg + 1, n_seg), "tp": across_two},
            device_id_type=MESH,
        )

    def rest_ahead(at):
        return pltpu.make_async_remote_copy(
            src_ref=final.at[pl.ds(at * piece, piece)],
            dst_ref=from_behind.at[at],
            send_sem=z_send.at[at],
            recv_sem=z_recv.at[at],
            device_id={"segment": lax.rem(seg + 1, n_seg)},
            device_id_type=MESH,
        )

    def hand(at):
        band = pl.ds(at * piece, piece)
        return pltpu.make_async_remote_copy(
            src_ref=final.at[band],
            dst_ref=out_ref.at[0, band],
            send_sem=z_send.at[at],
            recv_sem=z_recv.at[at],
            device_id={"segment": lax.rem(seg + 1, n_seg)},
            device_id_type=MESH,
        )

    f32 = jnp.float32
    for step in range(4):
        mirrored = 3 - step
        low = pl.multiple_of((mirrored + half * (3 - 2 * mirrored)) * cols, cols)
        share = jnp.dot(attn[...], wo[:, pl.ds(low, cols)], preferred_element_type=f32)
        own[step] = share
        if step < 3:

            @pl.when(at_end)
            def _():
                part[step] = share.astype(jnp.bfloat16)
                direct = (bands, near, 0)[step]
                for at in range(direct):
                    to_inner(step, at).start()
                if direct < bands:

                    @pl.when(ahead_too)
                    def _():
                        for at in range(direct, bands):
                            (skip_far if step == 1 else skip_ahead)(at).start()

                    @pl.when(jnp.logical_not(ahead_too))
                    def _():
                        for at in range(direct, bands):
                            to_inner(step, at).start()

    def finish(at, terms):
        band = slice(at * piece, (at + 1) * piece)
        total = terms[0][band]
        for term in terms[1:]:
            total = total + term[band].astype(f32)
        final[band] = total.astype(jnp.bfloat16)
        hand(at).start()

    def add_on(index, at, mine, landed):
        band = slice(at * piece, (at + 1) * piece)
        part[index, band] = (mine[band] + landed[band].astype(f32)).astype(jnp.bfloat16)

    @pl.when(at_end)
    def _():
        for at in range(bands):
            to_end(at).wait_recv()
            finish(at, [own.at[3], from_inner.at[0]])
        for step in range(3):
            for at in range(bands):
                to_inner(step, at).wait_send()
        for at in range(bands):
            hand(at).wait()

    @pl.when(jnp.logical_not(at_end))
    def _():
        for at in range(bands):
            to_inner(0, at).wait_recv()
            add_on(0, at, own.at[0], from_outer.at[0])
            over_middle(0, at).start()
        for at in range(bands):
            over_middle(0, at).wait_recv()
            add_on(2, at, own.at[3], from_inner.at[0])
            to_end(at).start()
            if at < near:
                to_inner(1, at).wait_recv()
                add_on(1, at, own.at[1], from_outer.at[1])
                over_middle(1, at).start()
            else:

                @pl.when(ahead_too)
                def _():
                    band = slice(at * piece, (at + 1) * piece)
                    part[1, band] = own[1, band].astype(jnp.bfloat16)
                    over_middle(1, at).start()

                @pl.when(jnp.logical_not(ahead_too))
                def _():
                    to_inner(1, at).wait_recv()
                    add_on(1, at, own.at[1], from_outer.at[1])
                    over_middle(1, at).start()

        @pl.when(ahead_too)
        def _():
            for at in range(bands):
                over_middle(1, at).wait_recv()
                band = slice(at * piece, (at + 1) * piece)
                rest = own[2, band] + from_inner[1, band].astype(f32)
                final[band] = rest.astype(jnp.bfloat16)
                rest_ahead(at).start()

        @pl.when(jnp.logical_not(ahead_too))
        def _():
            for at in range(bands):
                to_inner(2, at).wait_recv()
                over_middle(1, at).wait_recv()
                finish(at, [own.at[2], from_outer.at[2], from_inner.at[1]])

        for at in range(bands):
            over_middle(0, at).wait_send()
            over_middle(1, at).wait_send()
            to_end(at).wait_send()
        for at in range(bands):
            hand(at).wait_send()

        @pl.when(from_last)
        def _():
            for at in range(bands):
                rest_ahead(at).wait_recv()
                skip_ahead(at).wait_recv()
                band = slice(at * piece, (at + 1) * piece)
                total = from_behind[at].astype(f32) + from_mate[at].astype(f32)
                if at >= near:
                    skip_far(at).wait_recv()
                    total = total + from_far[at - near].astype(f32)
                out_ref[0, band] = total.astype(jnp.bfloat16)

        @pl.when(jnp.logical_not(from_last))
        def _():
            for at in range(bands):
                hand(at).wait_recv()

    for part_at in range(2 * groups):
        send_kv(0, 2, part_at, partner, 0).wait_send()
        send_kv(0, 1, part_at, partner, 1).wait_send()
        send_kv(2, 1, part_at, partner, 2).wait_send()


def solution(mesh):
    n_seg, n_ctx, n_tp = mesh.shape["segment"], mesh.shape["ctx"], mesh.shape["tp"]

    def body(hidden_in, norm_gain, query_weight, keyval_weight, output_weight, windows):
        rows, width = hidden_in.shape[1:]
        heads = query_weight.shape[2] // HD
        cols = output_weight.shape[2] // n_tp
        groups = keyval_weight.shape[2] // (2 * HD)
        bands = rows // PIECE
        half = HD // 2
        inverse = 10000.0 ** (-np.arange(half) / half)
        inverse = jnp.asarray(np.tile(inverse, 2)[None, :], dtype=jnp.float32)
        bf16 = jnp.bfloat16
        vmem = pl.BlockSpec(memory_space=pltpu.VMEM)
        hbm = pl.BlockSpec(memory_space=pl.ANY)
        return pl.pallas_call(
            functools.partial(block_kernel, n_seg, n_ctx, n_tp, PIECE),
            out_shape=pltpu.VMEM((1, rows, cols), bf16),
            in_specs=[pl.BlockSpec(memory_space=pltpu.SMEM)] + [hbm] * 6,
            out_specs=vmem,
            scratch_shapes=[
                pltpu.VMEM((1, width), bf16),
                pltpu.VMEM((1, HD), jnp.float32),
                pltpu.VMEM((rows, width), bf16),
                pltpu.VMEM(keyval_weight.shape[1:], bf16),
                pltpu.VMEM(query_weight.shape[1:], bf16),
                pltpu.VMEM(output_weight.shape[1:], bf16),
                pltpu.VMEM((rows, width), bf16),
                pltpu.VMEM((4, 2 * groups, rows, HD), bf16),
                pltpu.VMEM((heads, rows, HD), bf16),
                pltpu.VMEM((heads, 4, rows, HD), bf16),
                pltpu.VMEM((rows, heads * HD), bf16),
                pltpu.VMEM((4, rows, HD), jnp.float32),
                pltpu.VMEM((4, rows, cols), jnp.float32),
                pltpu.VMEM((3, rows, cols), bf16),
                pltpu.VMEM((3, rows, cols), bf16),
                pltpu.VMEM((2, rows, cols), bf16),
                pltpu.VMEM((FAR, PIECE, cols), bf16),
                pltpu.VMEM((bands, PIECE, cols), bf16),
                pltpu.VMEM((bands, PIECE, cols), bf16),
                pltpu.VMEM((rows, cols), bf16),
                pltpu.SemaphoreType.DMA((5 + DEPTHS,)),
                pltpu.SemaphoreType.DMA((3, 2 * groups)),
                pltpu.SemaphoreType.DMA((4, 2 * groups)),
                pltpu.SemaphoreType.DMA((3, bands)),
                pltpu.SemaphoreType.DMA((3, bands)),
                pltpu.SemaphoreType.DMA((2, bands)),
                pltpu.SemaphoreType.DMA((FAR,)),
                pltpu.SemaphoreType.DMA((bands,)),
                pltpu.SemaphoreType.DMA((bands,)),
                pltpu.SemaphoreType.DMA((bands,)),
            ],
            compiler_params=pltpu.CompilerParams(
                collective_id=0, has_side_effects=True, vmem_limit_bytes=56 * 1024 * 1024
            ),
        )(
            windows,
            norm_gain,
            inverse,
            hidden_in,
            keyval_weight,
            query_weight,
            output_weight,
        )

    in_specs = (
        P("segment", "ctx", None),
        P("segment", None),
        P("segment", None, "tp"),
        P("segment", None, "tp"),
        P("segment", "tp", None),
        P("segment"),
    )
    out_specs = P("segment", "ctx", "tp")
    return jax.shard_map(body, mesh=mesh, in_specs=in_specs, out_specs=out_specs, check_vma=False)
```
